32 devices in a mesh: groups: 2 (over y), seq: 4 (over z), head: 4 (over x, core).
Axes of the slice: x: 2, y: 2, z: 4, core: 2. Of those that a mesh axis runs over, the one named last changes fastest.
Arguments:
- xs: bfloat16 [4, 256, 8192], P('groups', 'seq', 'head'), parts along dimension 0, may hold values from -6 to 6
- gate_z: bfloat16 [4, 256, 8192], P('groups', 'seq', 'head'), parts along dimension 0, may hold values from -6 to 6
- dt_raw: float32 [4, 256, 128], P('groups', 'seq', 'head'), parts along dimension 0, as said below
- a_log: float32 [128], P('head'), as said below
- b_in: bfloat16 [4, 256, 1024], P('groups', 'seq', 'head'), parts along dimension 0, may hold values from -6 to 6
- c_in: bfloat16 [4, 256, 1024], P('groups', 'seq', 'head'), parts along dimension 0, may hold values from -6 to 6
- norm_gain: float32 [8192], P('head'), may hold values from 0.25 to 1.75
- w_out: bfloat16 [8192, 2048], P('head'), may hold values from -0.0625 to 0.0625
Outputs:
- projected: bfloat16 [4, 256, 2048], P('groups', 'seq', 'head'), parts along dimension 0
The draws below stay inside these ranges and needn't reach their ends.
There are 2 independent parts, one for each index of `groups`. The reference program is written for one: setup_inputs(seed, part) draws one part's arguments, and reference() takes and returns one part's arrays. A program takes and returns all parts, laid end to end along the dimension named above; an argument that names none is the same for every part. Nothing has to cross between parts.
Inputs may be any that keep to these rules, and one draw needn't show every extreme that they name: exp(a_log) lies between 0.15 / 256 and 1 / 30. softplus(dt_raw) lies between 0.25 and 1.4 * 256.
All inputs are finite; a program needn't handle non-finite values.
Results may differ from the reference program's by a relative error of at most 0.0057.
Values sent between devices are 32-bit elements; how exact they have to be, the bound alone decides.
No kernel may reach another device: no remote copies, remote signals or barrier semaphores. Data moves between devices by JAX's collectives and lax.ppermute only.
A program may use at most 192 MiB of HBM per device.

```python
import jax
import jax.numpy as jnp
from jax import lax

HEADS = 128
HEAD_DIM = 64
NS = 128
NG = 8
D_OUT = 2048
SPAN = 64
SEQUENCE_COUNT = 2
SEQUENCE_LENGTH = 256
INNER = 8192


def draw_a_log(key, part):
    k_pick, k_fast, k_slow = jax.random.split(key, 3)
    slow_share = 0.5
    is_slow = jax.random.uniform(k_pick, (HEADS,)) < slow_share
    fast_rate = jnp.exp(jax.random.uniform(k_fast, (HEADS,), minval=jnp.log(1.0 / 50.0), maxval=jnp.log(1.0 / 30.0)))
    slow_rate = jnp.exp(jax.random.uniform(k_slow, (HEADS,), minval=jnp.log(0.15 / SEQUENCE_LENGTH), maxval=jnp.log(0.5 / SEQUENCE_LENGTH)))
    return jnp.log(jnp.where(is_slow, slow_rate, fast_rate)).astype(jnp.float32)


def draw_dt_raw(key, part):
    base_random_key, block_random_key, spike_random_key = jax.random.split(key, 3)
    base_step = jnp.exp(jax.random.uniform(base_random_key, (SEQUENCE_COUNT, SEQUENCE_LENGTH, HEADS), minval=jnp.log(0.5), maxval=jnp.log(2.0)))
    blocks = SEQUENCE_LENGTH // SPAN
    block_scale = jnp.exp(jax.random.uniform(block_random_key, (SEQUENCE_COUNT, blocks, 1, HEADS), minval=jnp.log(0.5), maxval=jnp.log(2.0)))
    block_scale = jnp.broadcast_to(block_scale, (SEQUENCE_COUNT, blocks, SPAN, HEADS)).reshape(SEQUENCE_COUNT, SEQUENCE_LENGTH, HEADS)
    spike_position = jax.random.randint(spike_random_key, (SEQUENCE_COUNT, 2), 0, SEQUENCE_LENGTH)
    locations = jnp.any(jnp.arange(SEQUENCE_LENGTH)[None, :, None] == spike_position[:, None, :], axis=-1)
    step_size = jnp.where(locations[..., None], 1.4 * SEQUENCE_LENGTH, base_step * block_scale)
    return (step_size + jnp.log(-jnp.expm1(-step_size))).astype(jnp.float32)


def block_levels(rng, dims, cuts, low, high):
    loudness, own = 1.0, jax.random.fold_in(rng, 6)
    for axis_at, shards_of in cuts:
        heights = jnp.exp(jax.random.uniform(jax.random.fold_in(own, axis_at), (shards_of,), jnp.float32, low / len(cuts), high / len(cuts)))
        loudness = loudness * jnp.repeat(heights, dims[axis_at] // shards_of).reshape([-1 if axis == axis_at else 1 for axis in range(len(dims))])
    return loudness


def bell_draw(own_key, extent, spread, most, cuts=(), held_as=jnp.bfloat16):
    drawn = jax.random.normal(own_key, extent, jnp.float32) * spread
    if len(cuts) > 0:
        drawn = block_levels(own_key, extent, cuts, -0.22, 0.18) * drawn
    return jnp.clip(drawn, min=-most, max=most).astype(held_as)


def setup_inputs(seed: int = 0, part: int = 0) -> dict:
    streams_of = jax.random.split(jax.random.key(seed), 9)
    part_keys = jax.random.split(jax.random.fold_in(streams_of[8], part), 9)
    return {
        "xs": bell_draw(part_keys[0], (SEQUENCE_COUNT, SEQUENCE_LENGTH, INNER), 1.0, 6.0, ((1, 4), (2, 4))),
        "gate_z": bell_draw(part_keys[1], (SEQUENCE_COUNT, SEQUENCE_LENGTH, INNER), 1.0, 6.0, ((1, 4), (2, 4))),
        "dt_raw": draw_dt_raw(jax.random.fold_in(jax.random.fold_in(streams_of[8], part), 71), part),
        "a_log": draw_a_log(jax.random.fold_in(streams_of[8], 71), part),
        "b_in": bell_draw(part_keys[4], (SEQUENCE_COUNT, SEQUENCE_LENGTH, NG * NS), 1.0, 6.0, ((1, 4), (2, 4))),
        "c_in": bell_draw(part_keys[5], (SEQUENCE_COUNT, SEQUENCE_LENGTH, NG * NS), 1.0, 6.0, ((1, 4), (2, 4))),
        "norm_gain": jnp.clip(1.0 + 0.15 * jax.random.normal(streams_of[6], (INNER,), jnp.float32), 0.25, 1.75),
        "w_out": bell_draw(streams_of[7], (INNER, D_OUT), INNER ** -0.5, 0.0625, ((0, 4),)),
    }


EPSILON = 1e-05
STEP_CAP = 4.0

def reference(xs, gate_z, dt_raw, a_log, b_in, c_in, norm_gain, w_out):
    per_group = HEADS // NG
    blocks = SEQUENCE_LENGTH // SPAN
    step_size = jax.nn.softplus(dt_raw)
    log_decay = -jnp.exp(a_log) * step_size
    weight_in = jnp.minimum(step_size, STEP_CAP)

    def blocked(values_in, tail_shape):
        return jnp.moveaxis(values_in.reshape((SEQUENCE_COUNT, blocks, SPAN) + tail_shape), 1, 0)
    x_blocks = blocked(xs, (NG, per_group, HEAD_DIM))
    z_blocks = blocked(gate_z, (NG, per_group, HEAD_DIM))
    decay_blocks = blocked(log_decay, (NG, per_group))
    input_blocks = blocked(weight_in, (NG, per_group))
    b_blocks = blocked(b_in, (NG, NS))
    c_blocks = blocked(c_in, (NG, NS))
    causal = jnp.arange(SPAN)[:, None] >= jnp.arange(SPAN)[None, :]
    gain_groups = norm_gain.reshape(NG, per_group * HEAD_DIM)

    def one_block(carry_state, inputs):
        x_part, z_part, decay_part, input_part, b_part, c_part = inputs
        cumulative = jnp.cumsum(decay_part, axis=1)
        cumul_t = jnp.moveaxis(cumulative, 1, 3)
        input_t = jnp.moveaxis(input_part, 1, 3)
        scores = jnp.einsum('stgn,sugn->sgtu', c_part.astype(jnp.float32), b_part.astype(jnp.float32))
        differ = cumul_t[..., :, None] - cumul_t[..., None, :]
        within = jnp.where(causal, jnp.exp(jnp.where(causal, differ, 0.0)), 0.0) * input_t[..., None, :]
        mixing = (within * scores[:, :, None]).astype(jnp.bfloat16)
        y_intra = jnp.einsum('sgptu,sugpd->stgpd', mixing.astype(jnp.float32), x_part.astype(jnp.float32))
        block_total = cumul_t[..., -1:]
        to_end = jnp.exp(block_total - cumul_t) * input_t
        weighted = (x_part.astype(jnp.float32) * jnp.moveaxis(to_end, 3, 1)[..., None]).astype(jnp.bfloat16)
        block_state = jnp.einsum('sugpd,sugn->sgpdn', weighted.astype(jnp.float32), b_part.astype(jnp.float32))
        y_inter = jnp.exp(cumulative)[..., None] * jnp.einsum('stgn,sgpdn->stgpd', c_part.astype(jnp.float32), carry_state, precision=lax.Precision.HIGHEST)
        new_state = jnp.exp(block_total)[..., None] * carry_state + block_state
        gated_out = (y_intra + y_inter) * jax.nn.silu(z_part.astype(jnp.float32))
        gated_out = gated_out.reshape(SEQUENCE_COUNT, SPAN, NG, per_group * HEAD_DIM)
        square = lax.optimization_barrier(jnp.mean(gated_out * gated_out, axis=-1, keepdims=True))
        normed = (gated_out * lax.rsqrt(square + EPSILON) * gain_groups).astype(jnp.bfloat16)
        return (new_state, normed.reshape(SEQUENCE_COUNT, SPAN, HEADS * HEAD_DIM))
    initial = jnp.zeros((SEQUENCE_COUNT, NG, per_group, HEAD_DIM, NS), jnp.float32)
    _, normed = lax.scan(one_block, initial, (x_blocks, z_blocks, decay_blocks, input_blocks, b_blocks, c_blocks))
    normed = jnp.moveaxis(normed, 0, 1).reshape(SEQUENCE_COUNT * SEQUENCE_LENGTH, HEADS * HEAD_DIM)
    projected = jnp.dot(normed, w_out, preferred_element_type=jnp.float32)
    return projected.astype(jnp.bfloat16).reshape(SEQUENCE_COUNT, SEQUENCE_LENGTH, D_OUT)
```

```python
import functools

import jax
import jax.numpy as jnp
from jax import lax
from jax.experimental import pallas as pl
from jax.experimental.pallas import tpu as pltpu
from jax.sharding import PartitionSpec as P

HEAD_DIM = 64
NS = 128
SPAN = 64


EPSILON = 1e-05
STEP_CAP = 4.0
F32, BF16 = jnp.float32, jnp.bfloat16
VMEM = pl.BlockSpec(memory_space=pltpu.VMEM)


def dot(a, b):
    return jnp.dot(a, b, preferred_element_type=F32)


def dot_t(a, b):
    return lax.dot_general(a, b, (((1,), (1,)), ((), ())), preferred_element_type=F32)


def iota(shape, axis):
    return lax.broadcasted_iota(jnp.int32, shape, axis)


def split(v, parts):
    out = []
    for _ in range(parts):
        out.append(v.astype(BF16))
        v = v - out[-1].astype(F32)
    return out


def spread(v, channels):
    rows, heads = v.shape
    shape = (heads, channels)
    one = (lax.div(iota(shape, 1), HEAD_DIM) == iota(shape, 0)).astype(BF16)
    out = dot(jnp.concatenate(split(v, 3), 0), one)
    return out[:rows] + out[rows : 2 * rows] + out[2 * rows :]


def prelude_kernel(seqs, groups, x_ref, dt_ref, rate_ref, b_ref, c_ref, *outs):
    packs, (cpack_ref, cum_ref, win_ref, etot_ref) = outs[: seqs * groups], outs[seqs * groups :]
    rows, channels = x_ref.shape
    span, width = rows // seqs, channels // groups
    dt = dt_ref[...]
    step = jnp.maximum(dt, 0.0) + jnp.log1p(jnp.exp(-jnp.abs(dt)))
    decay = -jnp.exp(rate_ref[...]) * step
    win = jnp.minimum(step, STEP_CAP)
    i, j = iota((rows, rows), 0), iota((rows, rows), 1)
    same = lax.div(i, span) == lax.div(j, span)
    upto = (same & (j <= i)).astype(BF16)
    after = (same & (j > i)).astype(BF16)
    pieces = split(decay, 3)
    cum_ref[...] = sum(dot(upto, piece) for piece in pieces)
    left = sum(dot(after, piece) for piece in pieces)
    win_ref[...] = win
    weighted = (x_ref[...].astype(F32) * spread(jnp.exp(left) * win, channels)).astype(BF16)
    total = [jnp.sum(decay[s * span : (s + 1) * span], axis=0, keepdims=True) for s in range(seqs)]
    total = jnp.concatenate([jnp.broadcast_to(t, (8, t.shape[1])) for t in total], 0)
    etot = spread(jnp.exp(total), channels)
    etot_ref[...] = etot
    for s in range(seqs):
        at = slice(s * span, (s + 1) * span)
        for g in range(groups):
            pack = packs[s * groups + g]
            pack[:, :width] = weighted[at, g * width : (g + 1) * width].astype(F32)
            pack[:, width:] = b_ref[at, g * NS : (g + 1) * NS].astype(F32)
        lanes = groups * NS
        extra = channels // lanes
        base = s * (span + extra)
        cpack_ref[base : base + span, :] = c_ref[at, :].astype(F32)
        for k in range(extra):
            cpack_ref[base + span + k : base + span + k + 1, :] = etot[
                s * 8 : s * 8 + 1, k * lanes : (k + 1) * lanes
            ]


def local_kernel(seqs, groups, x_ref, z_ref, b_ref, c_ref, cum_ref, win_ref, base_ref, slope_ref):
    rows, channels = x_ref.shape
    span, width = rows // seqs, channels // groups
    both = spread(jnp.concatenate([cum_ref[...], win_ref[...]], 0), channels)
    t, u = iota((span, channels), 0), lax.rem(iota((span, channels), 1), span)
    four = 4 * HEAD_DIM
    own = lax.div(iota((four, four), 0), HEAD_DIM) == lax.div(iota((four, four), 1), HEAD_DIM)
    for s in range(seqs):
        at = slice(s * span, (s + 1) * span)
        cum, win = both[at], both[rows + s * span : rows + (s + 1) * span]
        cum_u = jnp.sum(jnp.where(t == u, cum, 0.0), axis=0, keepdims=True)
        win_u = jnp.sum(jnp.where(t == u, win, 0.0), axis=0, keepdims=True)
        within = jnp.exp(jnp.where(t >= u, cum - cum_u, -1e30)) * win_u
        z = z_ref[at, :].astype(F32)
        gate = z / (1.0 + jnp.exp(-z))
        slope_ref[at, :] = jnp.exp(cum) * gate
        for g in range(groups):
            state = slice(g * NS, (g + 1) * NS)
            scores = dot_t(c_ref[at, state], b_ref[at, state])
            scores = jnp.concatenate([scores, scores], 1)
            for q in range(width // four):
                lanes = slice(g * width + q * four, g * width + (q + 1) * four)
                mixing = (within[:, lanes] * jnp.concatenate([scores, scores], 1)).astype(BF16)
                x = jnp.concatenate([x_ref[at, lanes]] * 4, 0)
                x = jnp.where(own, x, jnp.zeros_like(x))
                base_ref[at, lanes] = dot(mixing, x) * gate[:, lanes]


def far_kernel(s, g, groups, c_ref, c2_ref, c3_ref, pack_ref, got_ref, etot_ref, own_ref, y2_ref, y3_ref):
    span = pack_ref.shape[0]
    width = pack_ref.shape[1] - NS
    lanes = groups * NS
    extra = (c2_ref.shape[0] - 2 * 0) // (c_ref.shape[0] // span) - span
    state = slice(g * NS, (g + 1) * NS)
    top = s * (span + extra)
    queries = [
        c_ref[s * span : (s + 1) * span, state],
        c2_ref[top : top + span, state].astype(BF16),
        c3_ref[top : top + span, state].astype(BF16),
    ]
    queries = jnp.concatenate(queries, 0)

    def through(queries, ref):
        scores = dot_t(queries, ref[:, width:].astype(BF16))
        values = ref[:, :width].astype(BF16)
        return sum(dot(piece, values) for piece in split(scores, 2))

    got = through(queries, got_ref)
    own_ref[...] = got[:span]
    etot = etot_ref[s * 8 : s * 8 + 1, g * width : (g + 1) * width]
    both = through(queries[span:], pack_ref) + etot * got[span:]
    y2_ref[...] = both[:span]
    for k in range(width // lanes):
        row = top + span + g * (width // lanes) + k
        at = slice(k * lanes, (k + 1) * lanes)
        y3_ref[:, at] = both[span:, at] * c2_ref[row : row + 1, :]


def finish_kernel(parts, me_ref, base_ref, slope_ref, own_ref, r2_ref, r3_ref, gain_ref, w_ref, *refs):
    outs = refs[-parts:]
    before = refs[: len(refs) - parts]
    gated = base_ref[...] + slope_ref[...] * (own_ref[...] + r2_ref[...] + r3_ref[...])
    square = jnp.mean(gated * gated, axis=-1, keepdims=True)
    normed = (gated * lax.rsqrt(square + EPSILON) * gain_ref[...]).astype(BF16)
    columns = w_ref.shape[1] // parts
    for r in range(parts):
        at = pl.multiple_of(lax.bitwise_xor(me_ref[0], r) * columns, columns)
        term = dot(normed, w_ref[:, pl.ds(at, columns)])
        outs[r][...] = term + before[r][...] if before else term


def call(kernel, outs, args, flops=0, **kw):
    shapes = [jax.ShapeDtypeStruct(s, F32) for s in outs]
    size = sum(a.size * a.dtype.itemsize for a in args) + sum(4 * s.size for s in shapes)
    cost = pl.CostEstimate(flops=flops, bytes_accessed=size, transcendentals=0)
    return pl.pallas_call(
        kernel,
        out_shape=shapes,
        in_specs=[VMEM] * len(args),
        out_specs=[VMEM] * len(shapes),
        cost_estimate=cost,
        **kw,
    )(*args)


def four_body(xs, gate_z, dt_raw, a_log, b_in, c_in, norm_gain, w_out):
    seqs, span, channels = xs.shape
    heads = dt_raw.shape[2]
    groups = b_in.shape[2] // NS
    width = channels // groups
    rows = seqs * span
    parts = lax.axis_size("head")
    columns = w_out.shape[1] // parts
    lanes = groups * NS
    x, z = xs.reshape(rows, channels), gate_z.reshape(rows, channels)
    b, c = b_in.reshape(rows, lanes), c_in.reshape(rows, lanes)
    dt = dt_raw.reshape(rows, heads)
    units = [(s, g) for s in range(seqs) for g in range(groups)]
    outs = [(span, width + NS)] * len(units)
    outs += [(seqs * (span + channels // lanes), lanes), (rows, heads), (rows, heads), (seqs * 8, channels)]
    out = call(
        functools.partial(prelude_kernel, seqs, groups), outs, (x, dt, a_log.reshape(1, heads), b, c)
    )
    packs, (cpack, cum, win, etot) = out[: len(units)], out[len(units) :]
    got = [lax.ppermute(packs[0], "seq", [(0, 1), (2, 3)])]
    c2 = lax.ppermute(cpack, "seq", [(2, 1)])
    c3 = lax.ppermute(cpack, "seq", [(3, 1)])
    got += [lax.ppermute(pack, "seq", [(0, 1), (2, 3)]) for pack in packs[1:]]
    base, slope = call(
        functools.partial(local_kernel, seqs, groups), [(rows, channels)] * 2, (x, z, b, c, cum, win)
    )
    gain = norm_gain.reshape(1, channels)
    me = lax.axis_index("head").reshape(1)
    far = []
    for k, (s, g) in enumerate(units):
        own, y2, y3 = call(
            functools.partial(far_kernel, s, g, groups),
            [(span, width)] * 3,
            (c, c2, c3, packs[k], got[k], etot),
        )
        far.append((own, lax.ppermute(y2, "seq", [(1, 2)]), lax.ppermute(y3, "seq", [(1, 3)])))
    result = []
    for s in range(seqs):
        terms = []
        for g in range(groups):
            block = pl.BlockSpec((span, width), lambda i, m, s=s, g=g: (s, g))
            whole = pl.BlockSpec((span, width), lambda i, m: (0, 0))
            piece = pl.BlockSpec((span, columns), lambda i, m: (0, 0))
            terms = pl.pallas_call(
                functools.partial(finish_kernel, parts),
                out_shape=[jax.ShapeDtypeStruct((span, columns), F32)] * parts,
                grid_spec=pltpu.PrefetchScalarGridSpec(
                    num_scalar_prefetch=1,
                    grid=(1,),
                    in_specs=[block, block, whole, whole, whole]
                    + [
                        pl.BlockSpec((1, width), lambda i, m, g=g: (0, g)),
                        pl.BlockSpec((width, w_out.shape[1]), lambda i, m, g=g: (g, 0)),
                    ]
                    + [piece] * len(terms),
                    out_specs=[piece] * parts,
                ),
            )(me, base, slope, *far[s * groups + g], gain, w_out, *terms)
        total = terms[0]
        for r in range(1, parts):
            total = total + lax.ppermute(terms[r], "head", [(i, i ^ r) for i in range(parts)])
        result.append(total.astype(BF16))
    return jnp.stack(result)


def carried_in(value, axis, combine, identity):
    peers, place = (lax.axis_size(axis), lax.axis_index(axis))
    everything = jax.tree.map(lambda part: lax.all_gather(part, axis), value)
    start = jax.tree.map(
        lambda part, zero: jnp.broadcast_to(jnp.asarray(zero, part.dtype), part.shape),
        value,
        identity,
    )

    def turn(k, before):
        reached = k < place
        new = combine(before, jax.tree.map(lambda part: part[k], everything))
        return jax.tree.map(lambda a, b: jnp.where(reached, a, b), new, before)

    return lax.fori_loop(0, peers, turn, start)


def body(xs, gate_z, dt_raw, a_log, b_in, c_in, norm_gain, w_out):
    seq_count, row_count, channels = xs.shape
    head_count = dt_raw.shape[2]
    group_count = b_in.shape[2] // NS
    per_group = head_count // group_count
    blocks = row_count // SPAN
    step_size = jax.nn.softplus(dt_raw)
    log_decay = -jnp.exp(a_log) * step_size
    weight_in = jnp.minimum(step_size, STEP_CAP)
    block_shape = (seq_count, blocks, SPAN, group_count, per_group, HEAD_DIM)
    x_parts = xs.reshape(block_shape)
    z_parts = gate_z.reshape(block_shape)
    decay_parts = log_decay.reshape(seq_count, blocks, SPAN, group_count, per_group)
    input_parts = weight_in.reshape(seq_count, blocks, SPAN, group_count, per_group)
    b_parts = b_in.reshape(seq_count, blocks, SPAN, group_count, NS)
    c_parts = c_in.reshape(seq_count, blocks, SPAN, group_count, NS)
    cumulative = jnp.cumsum(decay_parts, axis=2)
    cumul_t = jnp.moveaxis(cumulative, 2, 4)
    input_t = jnp.moveaxis(input_parts, 2, 4)
    causal = jnp.arange(SPAN)[:, None] >= jnp.arange(SPAN)[None, :]
    scores = jnp.einsum("sbtgn,sbugn->sbgtu", c_parts, b_parts, preferred_element_type=jnp.float32)
    differ = cumul_t[..., :, None] - cumul_t[..., None, :]
    within = jnp.where(causal, jnp.exp(jnp.where(causal, differ, 0.0)), 0.0) * input_t[..., None, :]
    mixing = (within * scores[:, :, :, None]).astype(jnp.bfloat16)
    y_intra = jnp.einsum(
        "sbgptu,sbugpd->sbtgpd", mixing, x_parts, preferred_element_type=jnp.float32
    )
    block_total = cumul_t[..., -1]
    to_end = jnp.exp(block_total[..., None] - cumul_t) * input_t
    weighted = (x_parts.astype(jnp.float32) * jnp.moveaxis(to_end, 4, 2)[..., None]).astype(
        jnp.bfloat16
    )
    block_states = jnp.einsum(
        "sbugpd,sbugn->sbgpdn", weighted, b_parts, preferred_element_type=jnp.float32
    )
    running = jnp.zeros((seq_count, group_count, per_group, HEAD_DIM, NS), jnp.float32)
    total_decay = jnp.zeros((seq_count, group_count, per_group), jnp.float32)
    entering = running
    before = total_decay
    running = jnp.exp(block_total[:, 0])[..., None, None] * running + block_states[:, 0]
    total_decay = block_total[:, 0]

    def combine(earlier, latter):
        return (
            earlier[0] + latter[0],
            jnp.exp(latter[0])[..., None, None] * earlier[1] + latter[1],
        )

    identity = (jnp.zeros_like(total_decay), jnp.zeros_like(running))
    _, carried = carried_in((total_decay, running), "seq", combine, identity)
    starts = jnp.stack([entering + jnp.exp(before)[..., None, None] * carried], axis=1)
    y_inter = jnp.exp(cumulative)[..., None] * jnp.einsum(
        "sbtgn,sbgpdn->sbtgpd", c_parts.astype(jnp.float32), starts, precision=lax.Precision.HIGHEST
    )
    gated_out = (y_intra + y_inter) * jax.nn.silu(z_parts.astype(jnp.float32))
    gated_out = gated_out.reshape(seq_count, row_count, group_count, per_group * HEAD_DIM)
    square = jnp.mean(gated_out * gated_out, axis=-1, keepdims=True)
    gain_groups = norm_gain.reshape(group_count, per_group * HEAD_DIM)
    normed = (gated_out * lax.rsqrt(square + EPSILON) * gain_groups).astype(jnp.bfloat16)
    normed = normed.reshape(seq_count * row_count, channels)
    partial_value = jnp.dot(normed, w_out, preferred_element_type=jnp.float32).reshape(
        seq_count, row_count, w_out.shape[1]
    )
    return lax.psum_scatter(partial_value, "head", scatter_dimension=2, tiled=True).astype(
        jnp.bfloat16
    )


def solution(mesh):
    in_specs = (
        P("groups", "seq", "head"),
        P("groups", "seq", "head"),
        P("groups", "seq", "head"),
        P("head"),
        P("groups", "seq", "head"),
        P("groups", "seq", "head"),
        P("head"),
        P("head", None),
    )
    out_specs = P("groups", "seq", "head")
    peers, parts = mesh.shape["seq"], mesh.shape["head"]
    step = four_body if peers == 4 and parts & (parts - 1) == 0 else body
    return jax.shard_map(step, mesh=mesh, in_specs=in_specs, out_specs=out_specs, check_vma=False)
```
